32 devices in a mesh: ctx: 8 (over z, core), tp: 4 (over y, x).
Axes of the slice: x: 2, y: 2, z: 4, core: 2. Of those that a mesh axis runs over, the one named last changes fastest.
Arguments:
- tokens: bfloat16 [4096, 4096], P(('ctx', 'tp')), may hold values from -6 to 6
- in_weight: bfloat16 [3, 4096, 2048], P(None, None, 'tp'), may hold values from -0.09375 to 0.09375
- short_taps: float32 [3, 3, 2048], P(None, None, 'tp'), may hold values from -3 to 3
- decay_rate: float32 [16, 2048], P(None, 'tp'), may hold values from 4.8828125e-05 to 0.0333333333
- residue: float32 [16, 2048], P(None, 'tp'), may hold values from -0.26 to 0.26
- skip_gain: float32 [2048], P('tp'), may hold values from -4 to 4
- grad_out: bfloat16 [4096, 2048], P('ctx', 'tp'), may hold values from -6 to 6
Outputs:
- mixed_out: bfloat16 [4096, 2048], P('ctx', 'tp')
- input_grad: bfloat16 [4096, 4096], P(('ctx', 'tp'))
The draws below stay inside these ranges and needn't reach their ends.
All inputs are finite; a program needn't handle non-finite values.
Results may differ from the reference program's by a relative error of at most 0.0065.
Values may be sent and summed in bfloat16 or wider, within the bound.
A program may use at most 192 MiB of HBM per device.

```python
import math
import jax
import jax.numpy as jnp
from jax import lax

D = 4096
CH = 2048
MODES = 16
SHORT = 3
TOKENS = 4096


def mode_table(key):
    folded = jax.random.fold_in(key, 11)
    subkeys = jax.random.split(folded, 4)
    fast_rate = jnp.exp(jax.random.uniform(subkeys[0], (MODES, CH), jnp.float32, math.log(1.0 / 50.0), math.log(1.0 / 30.0)))
    slow_rate = jnp.exp(jax.random.uniform(subkeys[1], (MODES, CH), jnp.float32, math.log(0.2 / TOKENS), math.log(2.0 / TOKENS)))
    fast_share = 0.5
    amplitude = jnp.clip(jax.random.normal(subkeys[3], (MODES, CH), jnp.float32), -4.0, 4.0)
    picked = jax.random.uniform(subkeys[2], (MODES, CH), jnp.float32) < fast_share
    decays = jnp.where(picked, fast_rate, slow_rate)
    weights = jnp.clip(amplitude * jnp.sqrt(2.0 * decays / MODES), -0.26, 0.26)
    return (decays, weights)


def draw_decay_rate(key, part):
    return mode_table(key)[0]


def draw_residue(key, part):
    return mode_table(key)[1]


def block_scale(own_key, shape, pieces, least, top_value):
    def one(dim, shards_of):
        steps = jax.random.uniform(jax.random.fold_in(jax.random.fold_in(own_key, 6), dim), (shards_of,), jnp.float32, least / len(pieces), top_value / len(pieces))
        return jnp.repeat(jnp.exp(steps), shape[dim] // shards_of).reshape((-1,) + (1,) * (len(shape) - dim - 1))

    factor_of = one(*pieces[0])
    for cut in pieces[1:]:
        factor_of = factor_of * one(*cut)
    return factor_of


def centred(stream_key, shape, scale, bound, shards=(), held_as=jnp.bfloat16):
    level = block_scale(stream_key, shape, shards, -0.22, 0.18) if shards else 1.0
    result = jax.random.normal(stream_key, shape, jnp.float32) * scale * level
    return jnp.minimum(jnp.maximum(result, -bound), bound).astype(held_as)


def setup_inputs(seed: int = 0) -> dict:
    keys = jax.random.split(jax.random.key(seed), 8)
    tokens = centred(keys[0], (TOKENS, D), 1.0, 6.0, ((0, 32),))
    in_weight = centred(keys[1], (3, D, CH), D ** -0.5, 0.09375, ((2, 4),))
    short_taps = centred(keys[2], (3, SHORT, CH), 0.6, 3.0, ((2, 4),), jnp.float32)
    decay_rate = draw_decay_rate(jax.random.fold_in(keys[7], 71), 0)
    residue = draw_residue(jax.random.fold_in(keys[7], 71), 0)
    skip_gain = centred(keys[5], (CH,), 1.0, 4.0, ((0, 4),), jnp.float32)
    grad_out = centred(keys[6], (TOKENS, CH), 1.0, 6.0, ((0, 8), (1, 4)))
    return {"tokens": tokens, "in_weight": in_weight, "short_taps": short_taps, "decay_rate": decay_rate, "residue": residue, "skip_gain": skip_gain, "grad_out": grad_out}


def reference(tokens, in_weight, short_taps, decay_rate, residue, skip_gain, grad_out):
    streams = jnp.stack([jnp.dot(tokens, in_weight[stream], preferred_element_type=jnp.float32).astype(jnp.bfloat16) for stream in range(3)], axis=1)
    tap_reach = SHORT - 1
    extended = jnp.concatenate([jnp.zeros((tap_reach, 3, CH), jnp.float32), streams.astype(jnp.float32)], axis=0)
    short_mixed = short_taps[:, 0][None] * extended[tap_reach:]
    for offset in range(1, tap_reach + 1):
        short_mixed = short_mixed + short_taps[:, offset][None] * extended[tap_reach - offset:tap_reach - offset + TOKENS]
    query_side = short_mixed[:, 0]
    key_side = short_mixed[:, 1]
    value_side = short_mixed[:, 2]
    product_in = key_side * value_side
    poles = jnp.exp(-decay_rate)

    def modal_step(state, column):
        state = poles * state + column[None]
        return state, jnp.sum(residue * state, axis=0)

    start_state = jnp.zeros((MODES, CH), jnp.float32)
    final_fwd, conv_out = lax.scan(modal_step, start_state, product_in)
    filtered = conv_out + skip_gain[None] * product_in
    mixed_out = (query_side * filtered).astype(jnp.bfloat16)
    upstream = grad_out.astype(jnp.float32)
    grad_query = upstream * filtered
    conv_grad = upstream * query_side
    final_bwd, back_conv = lax.scan(modal_step, start_state, conv_grad, reverse=True)
    grad_product = back_conv + skip_gain[None] * conv_grad
    stream_grads = jnp.stack([grad_query, grad_product * value_side, grad_product * key_side], axis=1)
    padded = jnp.concatenate([stream_grads, jnp.zeros((tap_reach, 3, CH), jnp.float32)], axis=0)
    grad_streams = short_taps[:, 0][None] * padded[:TOKENS]
    for offset in range(1, tap_reach + 1):
        grad_streams = grad_streams + short_taps[:, offset][None] * padded[offset:offset + TOKENS]
    grad_streams = grad_streams.astype(jnp.bfloat16)
    total = jnp.zeros((TOKENS, D), jnp.float32)
    for stream in range(3):
        total = total + jnp.dot(grad_streams[:, stream], in_weight[stream].T, preferred_element_type=jnp.float32)
    return mixed_out, total.astype(jnp.bfloat16)
```

```python
import functools

import jax
import jax.numpy as jnp
from jax import lax
from jax.experimental import pallas as pl
from jax.experimental.pallas import tpu as pltpu
from jax.sharding import PartitionSpec as P

exact_mode = lax.Precision.HIGHEST


def from_behind(value, axis, steps):
    count = lax.axis_size(axis)
    leading, last = (max(0, -steps), min(count, count - steps))
    return lax.ppermute(value, axis, [(source, source + steps) for source in range(leading, last)])


def modal_block(signal, log_pole, residue):
    length, channels = signal.shape
    sub_len = min(64, length)
    sub_count = length // sub_len
    offsets = jnp.arange(sub_len, dtype=jnp.float32)
    sections = signal.reshape(sub_count, sub_len, channels)
    powers = jnp.exp(log_pole[:, None, :] * offsets[None, :, None])
    filter_taps = jnp.sum(residue[:, None, :] * powers, axis=0)
    lag_index = jnp.arange(sub_len)[:, None] - jnp.arange(sub_len)[None, :]
    toeplitz = jnp.where((lag_index >= 0)[:, :, None], filter_taps[jnp.maximum(lag_index, 0)], 0.0)
    within = jnp.einsum("abc,kbc->kac", toeplitz, sections, precision=exact_mode)
    to_end = jnp.exp(log_pole[:, None, :] * (sub_len - 1.0 - offsets)[None, :, None])
    end_states = jnp.einsum("nbc,kbc->nkc", to_end, sections, precision=exact_mode)
    lag_blocks = jnp.arange(sub_count + 1)[:, None] - 1 - jnp.arange(sub_count)[None, :]
    valid_lag = lag_blocks >= 0
    lag_float = (jnp.maximum(lag_blocks, 0) * sub_len).astype(jnp.float32)
    decay_table = jnp.exp(log_pole[None, None] * lag_float[:, :, None, None])
    decay_table = jnp.where(valid_lag[:, :, None, None], decay_table, 0.0)
    carried = jnp.einsum("kmnc,nmc->nkc", decay_table, end_states, precision=exact_mode)
    stepped = residue[:, None, :] * jnp.exp(log_pole[:, None, :] * (offsets[None, :, None] + 1.0))
    output = within + jnp.einsum(
        "nac,nkc->kac", stepped, carried[:, :sub_count], precision=exact_mode
    )
    return (output.reshape(length, channels), carried[:, sub_count])


def carry_term(incoming, log_pole, residue, length):
    channels = incoming.shape[1]
    sub_len = min(64, length)
    sub_count = length // sub_len
    offsets = jnp.arange(sub_len, dtype=jnp.float32)
    stepped = residue[:, None, :] * jnp.exp(log_pole[:, None, :] * (offsets[None, :, None] + 1.0))
    block_starts = (jnp.arange(sub_count) * sub_len).astype(jnp.float32)
    start_states = incoming[:, None, :] * jnp.exp(
        log_pole[:, None, :] * block_starts[None, :, None]
    )
    output = jnp.einsum("nac,nkc->kac", stepped, start_states, precision=exact_mode)
    return output.reshape(length, channels)


def shards(tokens, in_weight, short_taps, decay_rate, residue, skip_gain, grad_out):
    width = in_weight.shape[2]
    weight_cat = jnp.concatenate([in_weight[0], in_weight[1], in_weight[2]], axis=1)
    streams = jnp.dot(
        lax.all_gather(tokens, "tp", axis=0, tiled=True),
        weight_cat,
        preferred_element_type=jnp.float32,
    ).astype(jnp.bfloat16)
    length = streams.shape[0]
    tap_reach = short_taps.shape[1] - 1
    taps_cat = jnp.concatenate([short_taps[0], short_taps[1], short_taps[2]], axis=1)
    before = from_behind(streams[length - tap_reach :], "ctx", 1)
    extended = jnp.concatenate([before, streams], axis=0).astype(jnp.float32)
    short_mixed = taps_cat[0][None] * extended[tap_reach:]
    for offset in range(1, tap_reach + 1):
        short_mixed = (
            short_mixed
            + taps_cat[offset][None] * extended[tap_reach - offset : tap_reach - offset + length]
        )
    query_side = short_mixed[:, :width]
    key_side = short_mixed[:, width : 2 * width]
    value_side = short_mixed[:, 2 * width :]
    product_in = key_side * value_side
    log_pole = -decay_rate
    forward_local, forward_sum = modal_block(product_in, log_pole, residue)
    upstream = grad_out.astype(jnp.float32)
    conv_grad = upstream * query_side
    backward_local, backward_sum = modal_block(conv_grad[::-1], log_pole, residue)
    position = lax.axis_index("ctx")
    summaries = (
        lax.all_gather(forward_sum[None], "ctx", axis=0, tiled=True),
        lax.all_gather(backward_sum[None], "ctx", axis=0, tiled=True),
    )
    block_index = jnp.arange(summaries[0].shape[0])
    earlier_gap = position - 1 - block_index
    later_gap = block_index - position - 1
    scale_fwd = (jnp.maximum(earlier_gap, 0) * length).astype(jnp.float32)
    scale_bwd = (jnp.maximum(later_gap, 0) * length).astype(jnp.float32)
    weight_fwd = jnp.where(
        (earlier_gap >= 0)[:, None, None], jnp.exp(log_pole[None] * scale_fwd[:, None, None]), 0.0
    )
    weight_bwd = jnp.where(
        (later_gap >= 0)[:, None, None], jnp.exp(log_pole[None] * scale_bwd[:, None, None]), 0.0
    )
    incoming_fwd = jnp.sum(weight_fwd * summaries[0], axis=0)
    incoming_bwd = jnp.sum(weight_bwd * summaries[1], axis=0)
    conv_out = forward_local + carry_term(incoming_fwd, log_pole, residue, length)
    back_conv = (backward_local + carry_term(incoming_bwd, log_pole, residue, length))[::-1]
    filtered = conv_out + skip_gain[None] * product_in
    result = (query_side * filtered).astype(jnp.bfloat16)
    grad_query = upstream * filtered
    grad_product = back_conv + skip_gain[None] * conv_grad
    stream_grads = jnp.concatenate(
        [grad_query, grad_product * value_side, grad_product * key_side], axis=1
    )
    after_rows = from_behind(stream_grads[:tap_reach], "ctx", -1)
    padded = jnp.concatenate([stream_grads, after_rows], axis=0)
    grad_streams = taps_cat[0][None] * padded[:length]
    for offset in range(1, tap_reach + 1):
        grad_streams = grad_streams + taps_cat[offset][None] * padded[offset : offset + length]
    grad_streams = grad_streams.astype(jnp.bfloat16)
    input_grad = lax.psum_scatter(
        jnp.einsum("rk,dk->rd", grad_streams, weight_cat, preferred_element_type=jnp.float32),
        "tp",
        scatter_dimension=0,
        tiled=True,
    )
    return (result, input_grad.astype(jnp.bfloat16))


MESH = pl.DeviceIdType.MESH
SUBLANES = 8
LANES = 128
ROWS = 32
VMEM_LIMIT = 60 * 1024 * 1024


def vmem_specs(count):
    return [pl.BlockSpec(memory_space=pltpu.VMEM)] * count


def square_partners():
    me = lax.axis_index("tp")
    y, x = me // 2, me % 2
    return me, y * 2 + (1 - x), (1 - y) * 2 + x, (1 - y) * 2 + (1 - x)


def greet(axis, partners):
    barrier = pltpu.get_barrier_semaphore()
    for partner in partners:
        pl.semaphore_signal(barrier, inc=1, device_id={axis: partner}, device_id_type=MESH)
    pl.semaphore_wait(barrier, len(partners))


def project_kernel(tok_ref, w_hbm, out_ref, held, w_buf, w_sem, send_sem, recv_sem):
    rows = tok_ref.shape[0]
    half = rows // 2
    width = w_hbm.shape[2]
    tile = w_buf.shape[2]
    per_stream = width // tile
    me, xn, yn, dg = square_partners()
    loads = []
    for part in range(3 * per_stream):
        stream, col = divmod(part, per_stream)
        load = pltpu.make_async_copy(
            w_hbm.at[stream, :, pl.ds(col * tile, tile)], w_buf.at[part], w_sem.at[part]
        )
        load.start()
        loads.append(load)
    greet("tp", (xn, yn))

    def send(index, source, slot, start, partner):
        return pltpu.make_async_remote_copy(
            src_ref=source,
            dst_ref=held.at[slot, pl.ds(start, half)],
            send_sem=send_sem.at[index],
            recv_sem=recv_sem.at[index],
            device_id={"tp": partner},
            device_id_type=MESH,
        )

    own_a, own_b = tok_ref.at[pl.ds(0, half)], tok_ref.at[pl.ds(half, half)]
    copies = [
        send(0, own_a, 0, 0, xn),
        send(1, own_b, 1, half, yn),
        send(2, own_b, 0, half, xn),
        send(3, own_a, 1, 0, yn),
        send(4, held.at[0, pl.ds(0, half)], 2, 0, yn),
        send(5, held.at[1, pl.ds(half, half)], 2, half, xn),
    ]
    for index in range(4):
        copies[index].start()

    def multiply(block, owner):
        start = pl.multiple_of(owner * rows, rows)

        @pl.loop(0, 3 * per_stream)
        def _(part):
            out_ref[part, pl.ds(start, rows), :] = jnp.dot(
                block[...], w_buf[part], preferred_element_type=jnp.float32
            ).astype(out_ref.dtype)

    for load in loads:
        load.wait()
    multiply(tok_ref, me)
    copies[0].wait_recv()
    copies[4].start()
    copies[1].wait_recv()
    copies[5].start()
    copies[2].wait_recv()
    multiply(held.at[0], xn)
    copies[3].wait_recv()
    multiply(held.at[1], yn)
    copies[4].wait_recv()
    copies[5].wait_recv()
    multiply(held.at[2], dg)
    for copy in copies:
        copy.wait_send()


def gather_project(tokens, in_weight):
    rows, depth = tokens.shape
    streams, _, width = in_weight.shape
    tile = min(256, width)
    parts = streams * (width // tile)
    return pl.pallas_call(
        project_kernel,
        out_shape=jax.ShapeDtypeStruct((parts, 4 * rows, tile), jnp.bfloat16),
        in_specs=[pl.BlockSpec(memory_space=pltpu.VMEM), pl.BlockSpec(memory_space=pl.ANY)],
        out_specs=pl.BlockSpec(memory_space=pltpu.VMEM),
        scratch_shapes=[
            pltpu.VMEM((3, rows, depth), jnp.bfloat16),
            pltpu.VMEM((parts, depth, tile), jnp.bfloat16),
            pltpu.SemaphoreType.DMA((parts,)),
            pltpu.SemaphoreType.DMA((6,)),
            pltpu.SemaphoreType.DMA((6,)),
        ],
        compiler_params=pltpu.CompilerParams(
            collective_id=0, has_side_effects=True, vmem_limit_bytes=VMEM_LIMIT
        ),
    )(tokens, in_weight)


def tree_sum(values):
    while len(values) > 1:
        values = [a + b for a, b in zip(values[::2], values[1::2])] + (
            [values[-1]] if len(values) % 2 else []
        )
    return values[0]


def middle_kernel(
    count, st_ref, taps_ref, rate_ref, res_ref, skip_ref, grad_ref, mixed_ref, gs_ref,
    ext, side, prod, cgrad, conv, back, sgrad, halo, pole, carry_f, carry_b,
    mine_f, mine_b, all_f, all_b, inc_f, inc_b,
    send_f, recv_f, send_b, recv_b, send_h, recv_h,
):
    parts, length, tile = st_ref.shape
    width = mixed_ref.shape[1]
    per_stream = width // tile
    modes = rate_ref.shape[0]
    section = length // SUBLANES
    chunks = length // ROWS
    me = lax.axis_index("ctx")
    after, prior = lax.rem(me + 1, count), lax.rem(me + count - 1, count)
    greet("ctx", [lax.rem(me + step, count) for step in range(1, count)])

    def neighbour(index, source, target, partner):
        return pltpu.make_async_remote_copy(
            src_ref=source,
            dst_ref=target,
            send_sem=send_h.at[index],
            recv_sem=recv_h.at[index],
            device_id={"ctx": partner},
            device_id_type=MESH,
        )

    first = neighbour(0, st_ref.at[:, pl.ds(length - 16, 16), :], halo, after)
    first.start()
    pole[...] = jnp.exp(-rate_ref[...])

    @pl.loop(0, chunks)
    def _(step):
        start = pl.multiple_of(step * ROWS, ROWS)
        for part in range(parts):
            ext[pl.ds(start + 8, ROWS), part * tile : (part + 1) * tile] = st_ref[
                part, pl.ds(start, ROWS), :
            ].astype(jnp.float32)

    first.wait_recv()
    keep = jnp.where(me > 0, 1.0, 0.0).astype(jnp.float32)
    for part in range(parts):
        ext[0:8, part * tile : (part + 1) * tile] = (
            halo[part].astype(jnp.float32)[8:16] * keep
        )

    @pl.loop(0, chunks)
    def _(step):
        start = pl.multiple_of(step * ROWS, ROWS)
        for col in range(0, width, LANES):
            lanes = slice(col, col + LANES)
            mixed = []
            for s in range(3):
                block = ext[pl.ds(start, ROWS + 8), s * width + col : s * width + col + LANES]
                value = taps_ref[s, 0:1, lanes] * block[8:]
                for j in range(1, 3):
                    value = value + taps_ref[s, j : j + 1, lanes] * block[8 - j : 8 - j + ROWS]
                side[s, pl.ds(start, ROWS), lanes] = value
                mixed.append(value)
            prod[col // LANES, pl.ds(start, ROWS), :] = mixed[1] * mixed[2]
            cgrad[col // LANES, pl.ds(start, ROWS), :] = (
                grad_ref[pl.ds(start, ROWS), lanes].astype(jnp.float32) * mixed[0]
            )

    tiles = width // LANES
    sub = lax.broadcasted_iota(jnp.int32, (SUBLANES, LANES), 0)

    def wide(ref, lanes):
        return [
            jnp.broadcast_to(ref[n : n + 1, lanes], (SUBLANES, LANES)) for n in range(modes)
        ]

    def local_scan(source, target, carry, mine, reverse):
        @pl.loop(0, tiles)
        def _(t):
            lanes = pl.ds(pl.multiple_of(t * LANES, LANES), LANES)
            p, r = wide(pole, lanes), wide(res_ref, lanes)

            def body(i, state):
                j = section - 1 - i if reverse else i
                x = source[t, pl.ds(j, SUBLANES, stride=section), :]
                state = [a * b + c * x for a, b, c in zip(p, state, r)]
                target[t, pl.ds(j, SUBLANES, stride=section), :] = tree_sum(state)
                return state

            zero = jnp.zeros((SUBLANES, LANES), jnp.float32)
            ends = lax.fori_loop(0, section, body, [zero] * modes, unroll=2)
            for n in range(modes):
                rate = rate_ref[n : n + 1, lanes]
                total = ends[n]
                for k in (1, 2, 4):
                    decay = jnp.exp(rate * (-1.0 * section * k))
                    moved = pltpu.roll(total, SUBLANES - k if reverse else k, 0)
                    inside = sub < SUBLANES - k if reverse else sub >= k
                    total = total + jnp.where(inside, decay * moved, 0.0)
                moved = pltpu.roll(total, SUBLANES - 1 if reverse else 1, 0)
                inside = sub < SUBLANES - 1 if reverse else sub >= 1
                carry[n, :, lanes] = jnp.where(inside, moved, 0.0)
                mine[n : n + 1, lanes] = total[0:1] if reverse else total[SUBLANES - 1 :]

    def summary(mine, table, send_sem, recv_sem, source, partner):
        return pltpu.make_async_remote_copy(
            src_ref=mine,
            dst_ref=table.at[source],
            send_sem=send_sem.at[partner],
            recv_sem=recv_sem.at[source],
            device_id={"ctx": partner},
            device_id_type=MESH,
        )

    forward = functools.partial(summary, mine_f, all_f, send_f, recv_f)
    backward = functools.partial(summary, mine_b, all_b, send_b, recv_b)

    local_scan(prod, conv, carry_f, mine_f, False)
    for other in range(count):

        @pl.when(other > me)
        def _(other=other):
            forward(me, other).start()

    local_scan(cgrad, back, carry_b, mine_b, True)
    for other in range(count):

        @pl.when(other < me)
        def _(other=other):
            backward(me, other).start()

    def add_carry(target, carry, incoming, reverse):
        @pl.loop(0, tiles)
        def _(t):
            lanes = pl.ds(pl.multiple_of(t * LANES, LANES), LANES)
            p = wide(pole, lanes)
            steps = (SUBLANES - 1 - sub if reverse else sub).astype(jnp.float32) * (-1.0 * section)
            state = [
                carry[n, :, lanes]
                + jnp.exp(rate_ref[n : n + 1, lanes] * steps) * incoming[n : n + 1, lanes]
                for n in range(modes)
            ]

            def body(i, state):
                j = section - 1 - i if reverse else i
                state = [a * b for a, b in zip(p, state)]
                place = pl.ds(j, SUBLANES, stride=section)
                target[t, place, :] = target[t, place, :] + tree_sum(state)
                return state

            lax.fori_loop(0, section, body, state, unroll=2)

    inc_f[...] = jnp.zeros_like(inc_f)
    for other in range(count):

        @pl.when(other < me)
        def _(other=other):
            forward(other, me).wait_recv()
            gap = ((other + 1 - me) * length).astype(jnp.float32)
            inc_f[...] += jnp.exp(rate_ref[...] * gap) * all_f[other]

    add_carry(conv, carry_f, inc_f, False)
    inc_b[...] = jnp.zeros_like(inc_b)
    for other in range(count):

        @pl.when(other > me)
        def _(other=other):
            backward(other, me).wait_recv()
            gap = ((me + 1 - other) * length).astype(jnp.float32)
            inc_b[...] += jnp.exp(rate_ref[...] * gap) * all_b[other]

    add_carry(back, carry_b, inc_b, True)

    def finish(start):
        for col in range(0, width, LANES):
            lanes = slice(col, col + LANES)
            rows = pl.ds(start, ROWS)
            skip = skip_ref[0:1, lanes]
            filtered = conv[col // LANES, rows, :] + skip * prod[col // LANES, rows, :]
            mixed_ref[rows, lanes] = (side[0, rows, lanes] * filtered).astype(mixed_ref.dtype)
            product = back[col // LANES, rows, :] + skip * cgrad[col // LANES, rows, :]
            upstream = grad_ref[rows, lanes].astype(jnp.float32)
            sgrad[rows, lanes] = upstream * filtered
            sgrad[rows, width + col : width + col + LANES] = product * side[2, rows, lanes]
            sgrad[rows, 2 * width + col : 2 * width + col + LANES] = product * side[1, rows, lanes]

    finish(0)
    last = neighbour(1, sgrad.at[pl.ds(0, 8)], sgrad.at[pl.ds(length, 8)], prior)
    last.start()

    @pl.loop(1, chunks)
    def _(step):
        finish(pl.multiple_of(step * ROWS, ROWS))

    def transpose_taps(start):
        for s in range(3):
            for col in range(0, width, LANES):
                lanes = slice(s * width + col, s * width + col + LANES)
                block = sgrad[pl.ds(start, ROWS + 8), lanes]
                value = taps_ref[s, 0:1, col : col + LANES] * block[:ROWS]
                for j in range(1, 3):
                    value = value + taps_ref[s, j : j + 1, col : col + LANES] * block[j : j + ROWS]
                gs_ref[pl.ds(start, ROWS), lanes] = value.astype(gs_ref.dtype)

    @pl.loop(0, chunks - 1)
    def _(step):
        transpose_taps(pl.multiple_of(step * ROWS, ROWS))

    last.wait_recv()

    @pl.when(me == count - 1)
    def _():
        sgrad[length : length + 8, :] = jnp.zeros((8, 3 * width), jnp.float32)

    transpose_taps(length - ROWS)
    first.wait_send()
    last.wait_send()
    for other in range(count):

        @pl.when(other > me)
        def _(other=other):
            forward(me, other).wait_send()

        @pl.when(other < me)
        def _(other=other):
            backward(me, other).wait_send()


def middle(streams, short_taps, decay_rate, residue, skip_gain, grad_out):
    count = lax.axis_size("ctx")
    parts, length, tile = streams.shape
    modes, width = decay_rate.shape
    f32 = jnp.float32
    table = pltpu.VMEM((modes, width), f32)
    tables = pltpu.VMEM((count, modes, width), f32)
    plane = pltpu.VMEM((width // LANES, length, LANES), f32)
    carry = pltpu.VMEM((modes, SUBLANES, width), f32)
    dma = pltpu.SemaphoreType.DMA
    return pl.pallas_call(
        functools.partial(middle_kernel, count),
        out_shape=(
            jax.ShapeDtypeStruct((length, width), jnp.bfloat16),
            jax.ShapeDtypeStruct((length, 3 * width), jnp.bfloat16),
        ),
        in_specs=vmem_specs(6),
        out_specs=tuple(vmem_specs(2)),
        scratch_shapes=[
            pltpu.VMEM((length + 8, 3 * width), f32),
            pltpu.VMEM((3, length, width), f32),
            plane, plane, plane, plane,
            pltpu.VMEM((length + 8, 3 * width), f32),
            pltpu.VMEM((parts, 16, tile), jnp.bfloat16),
            table, carry, carry, table, table, tables, tables, table, table,
            dma((count,)), dma((count,)), dma((count,)), dma((count,)), dma((2,)), dma((2,)),
        ],
        compiler_params=pltpu.CompilerParams(
            collective_id=1, has_side_effects=True, vmem_limit_bytes=VMEM_LIMIT
        ),
    )(streams, short_taps, decay_rate, residue, skip_gain[None], grad_out)


def scatter_kernel(gs_ref, w_hbm, out_ref, w_buf, out_buf, in_buf, own, w_sem, send_sem, recv_sem):
    rows, depth = out_ref.shape
    pieces, streams, cols, width = w_buf.shape
    half = pieces // 2
    me, xn, yn, dg = square_partners()

    def load(piece):
        return pltpu.make_async_copy(
            w_hbm.at[:, pl.ds(piece * cols, cols), :], w_buf.at[piece], w_sem.at[piece]
        )

    for piece in range(half):
        load(piece).start()
        load(half + piece).start()
    greet("tp", (xn, yn))

    def send(kind, piece, partner):
        return pltpu.make_async_remote_copy(
            src_ref=out_buf.at[kind, piece],
            dst_ref=in_buf.at[kind, piece],
            send_sem=send_sem.at[kind, piece],
            recv_sem=recv_sem.at[kind, piece],
            device_id={"tp": partner},
            device_id_type=MESH,
        )

    def partial(owner, piece):
        block = pl.ds(pl.multiple_of(owner * rows, rows), rows)
        total = None
        for s in range(streams):
            term = lax.dot_general(
                gs_ref[block, s * width : (s + 1) * width],
                w_buf[piece, s],
                (((1,), (1,)), ((), ())),
                preferred_element_type=jnp.float32,
            )
            total = term if total is None else total + term
        return total

    def emit(kind, piece, value, partner):
        out_buf[kind, piece] = value.astype(out_buf.dtype)
        send(kind, piece, partner).start()

    @pl.loop(0, half)
    def _(k):
        load(k).wait()
        emit(0, k, partial(dg, k), xn)
        load(half + k).wait()
        emit(0, half + k, partial(dg, half + k), yn)

    @pl.loop(0, half)
    def _(k):
        emit(1, k, partial(xn, k), xn)
        emit(2, half + k, partial(yn, half + k), yn)

    @pl.loop(0, half)
    def _(k):
        own_x, own_y = partial(xn, half + k), partial(yn, k)
        send(0, half + k, yn).wait_recv()
        emit(1, half + k, own_x + in_buf[0, half + k].astype(jnp.float32), xn)
        send(0, k, xn).wait_recv()
        emit(2, k, own_y + in_buf[0, k].astype(jnp.float32), yn)

    @pl.loop(0, pieces)
    def _(k):
        own[k] = partial(me, k)

    for k in [k + offset for k in range(half) for offset in (0, half)]:
        send(1, k, xn).wait_recv()
        send(2, k, yn).wait_recv()
        out_ref[:, k * cols : (k + 1) * cols] = (
            own[k] + in_buf[1, k].astype(jnp.float32) + in_buf[2, k].astype(jnp.float32)
        ).astype(out_ref.dtype)
    for k in range(pieces):
        send(0, k, xn if k < half else yn).wait_send()
        send(1, k, xn).wait_send()
        send(2, k, yn).wait_send()


def project_back(grad_streams, in_weight):
    length = grad_streams.shape[0]
    streams, depth, width = in_weight.shape
    rows, pieces = length // 4, 8
    cols = depth // pieces
    travelling = pltpu.VMEM((3, pieces, rows, cols), jnp.bfloat16)
    return pl.pallas_call(
        scatter_kernel,
        out_shape=jax.ShapeDtypeStruct((rows, depth), jnp.bfloat16),
        in_specs=[pl.BlockSpec(memory_space=pltpu.VMEM), pl.BlockSpec(memory_space=pl.ANY)],
        out_specs=pl.BlockSpec(memory_space=pltpu.VMEM),
        scratch_shapes=[
            pltpu.VMEM((pieces, streams, cols, width), jnp.bfloat16),
            travelling,
            travelling,
            pltpu.VMEM((pieces, rows, cols), jnp.float32),
            pltpu.SemaphoreType.DMA((pieces,)),
            pltpu.SemaphoreType.DMA((3, pieces)),
            pltpu.SemaphoreType.DMA((3, pieces)),
        ],
        compiler_params=pltpu.CompilerParams(
            collective_id=2, has_side_effects=True, vmem_limit_bytes=VMEM_LIMIT
        ),
    )(grad_streams, in_weight)


def square_shards(tokens, in_weight, short_taps, decay_rate, residue, skip_gain, grad_out):
    streams = gather_project(tokens, in_weight)
    mixed_out, grad_streams = middle(
        streams, short_taps, decay_rate, residue, skip_gain, grad_out
    )
    return mixed_out, project_back(grad_streams, in_weight)


def solution(mesh):
    in_specs = (
        P(("ctx", "tp"), None),
        P(None, None, "tp"),
        P(None, None, "tp"),
        P(None, "tp"),
        P(None, "tp"),
        P("tp"),
        P("ctx", "tp"),
    )
    out_specs = (P("ctx", "tp"), P(("ctx", "tp"), None))
    body = square_shards if mesh.shape["tp"] == 4 else shards
    return jax.shard_map(body, mesh=mesh, in_specs=in_specs, out_specs=out_specs, check_vma=False)
```

```python
import functools

import jax
import jax.numpy as jnp
from jax import lax
from jax.experimental import pallas as pl
from jax.experimental.pallas import tpu as pltpu
from jax.sharding import PartitionSpec as P

exact_mode = lax.Precision.HIGHEST


def from_behind(value, axis, steps):
    count = lax.axis_size(axis)
    leading, last = (max(0, -steps), min(count, count - steps))
    return lax.ppermute(value, axis, [(source, source + steps) for source in range(leading, last)])


def modal_block(signal, log_pole, residue):
    length, channels = signal.shape
    sub_len = min(64, length)
    sub_count = length // sub_len
    offsets = jnp.arange(sub_len, dtype=jnp.float32)
    sections = signal.reshape(sub_count, sub_len, channels)
    powers = jnp.exp(log_pole[:, None, :] * offsets[None, :, None])
    filter_taps = jnp.sum(residue[:, None, :] * powers, axis=0)
    lag_index = jnp.arange(sub_len)[:, None] - jnp.arange(sub_len)[None, :]
    toeplitz = jnp.where((lag_index >= 0)[:, :, None], filter_taps[jnp.maximum(lag_index, 0)], 0.0)
    within = jnp.einsum("abc,kbc->kac", toeplitz, sections, precision=exact_mode)
    to_end = jnp.exp(log_pole[:, None, :] * (sub_len - 1.0 - offsets)[None, :, None])
    end_states = jnp.einsum("nbc,kbc->nkc", to_end, sections, precision=exact_mode)
    lag_blocks = jnp.arange(sub_count + 1)[:, None] - 1 - jnp.arange(sub_count)[None, :]
    valid_lag = lag_blocks >= 0
    lag_float = (jnp.maximum(lag_blocks, 0) * sub_len).astype(jnp.float32)
    decay_table = jnp.exp(log_pole[None, None] * lag_float[:, :, None, None])
    decay_table = jnp.where(valid_lag[:, :, None, None], decay_table, 0.0)
    carried = jnp.einsum("kmnc,nmc->nkc", decay_table, end_states, precision=exact_mode)
    stepped = residue[:, None, :] * jnp.exp(log_pole[:, None, :] * (offsets[None, :, None] + 1.0))
    output = within + jnp.einsum(
        "nac,nkc->kac", stepped, carried[:, :sub_count], precision=exact_mode
    )
    return (output.reshape(length, channels), carried[:, sub_count])


def carry_term(incoming, log_pole, residue, length):
    channels = incoming.shape[1]
    sub_len = min(64, length)
    sub_count = length // sub_len
    offsets = jnp.arange(sub_len, dtype=jnp.float32)
    stepped = residue[:, None, :] * jnp.exp(log_pole[:, None, :] * (offsets[None, :, None] + 1.0))
    block_starts = (jnp.arange(sub_count) * sub_len).astype(jnp.float32)
    start_states = incoming[:, None, :] * jnp.exp(
        log_pole[:, None, :] * block_starts[None, :, None]
    )
    output = jnp.einsum("nac,nkc->kac", stepped, start_states, precision=exact_mode)
    return output.reshape(length, channels)


def shards(tokens, in_weight, short_taps, decay_rate, residue, skip_gain, grad_out):
    width = in_weight.shape[2]
    weight_cat = jnp.concatenate([in_weight[0], in_weight[1], in_weight[2]], axis=1)
    streams = jnp.dot(
        lax.all_gather(tokens, "tp", axis=0, tiled=True),
        weight_cat,
        preferred_element_type=jnp.float32,
    ).astype(jnp.bfloat16)
    length = streams.shape[0]
    tap_reach = short_taps.shape[1] - 1
    taps_cat = jnp.concatenate([short_taps[0], short_taps[1], short_taps[2]], axis=1)
    before = from_behind(streams[length - tap_reach :], "ctx", 1)
    extended = jnp.concatenate([before, streams], axis=0).astype(jnp.float32)
    short_mixed = taps_cat[0][None] * extended[tap_reach:]
    for offset in range(1, tap_reach + 1):
        short_mixed = (
            short_mixed
            + taps_cat[offset][None] * extended[tap_reach - offset : tap_reach - offset + length]
        )
    query_side = short_mixed[:, :width]
    key_side = short_mixed[:, width : 2 * width]
    value_side = short_mixed[:, 2 * width :]
    product_in = key_side * value_side
    log_pole = -decay_rate
    forward_local, forward_sum = modal_block(product_in, log_pole, residue)
    upstream = grad_out.astype(jnp.float32)
    conv_grad = upstream * query_side
    backward_local, backward_sum = modal_block(conv_grad[::-1], log_pole, residue)
    position = lax.axis_index("ctx")
    summaries = (
        lax.all_gather(forward_sum[None], "ctx", axis=0, tiled=True),
        lax.all_gather(backward_sum[None], "ctx", axis=0, tiled=True),
    )
    block_index = jnp.arange(summaries[0].shape[0])
    earlier_gap = position - 1 - block_index
    later_gap = block_index - position - 1
    scale_fwd = (jnp.maximum(earlier_gap, 0) * length).astype(jnp.float32)
    scale_bwd = (jnp.maximum(later_gap, 0) * length).astype(jnp.float32)
    weight_fwd = jnp.where(
        (earlier_gap >= 0)[:, None, None], jnp.exp(log_pole[None] * scale_fwd[:, None, None]), 0.0
    )
    weight_bwd = jnp.where(
        (later_gap >= 0)[:, None, None], jnp.exp(log_pole[None] * scale_bwd[:, None, None]), 0.0
    )
    incoming_fwd = jnp.sum(weight_fwd * summaries[0], axis=0)
    incoming_bwd = jnp.sum(weight_bwd * summaries[1], axis=0)
    conv_out = forward_local + carry_term(incoming_fwd, log_pole, residue, length)
    back_conv = (backward_local + carry_term(incoming_bwd, log_pole, residue, length))[::-1]
    filtered = conv_out + skip_gain[None] * product_in
    result = (query_side * filtered).astype(jnp.bfloat16)
    grad_query = upstream * filtered
    grad_product = back_conv + skip_gain[None] * conv_grad
    stream_grads = jnp.concatenate(
        [grad_query, grad_product * value_side, grad_product * key_side], axis=1
    )
    after_rows = from_behind(stream_grads[:tap_reach], "ctx", -1)
    padded = jnp.concatenate([stream_grads, after_rows], axis=0)
    grad_streams = taps_cat[0][None] * padded[:length]
    for offset in range(1, tap_reach + 1):
        grad_streams = grad_streams + taps_cat[offset][None] * padded[offset : offset + length]
    grad_streams = grad_streams.astype(jnp.bfloat16)
    input_grad = lax.psum_scatter(
        jnp.einsum("rk,dk->rd", grad_streams, weight_cat, preferred_element_type=jnp.float32),
        "tp",
        scatter_dimension=0,
        tiled=True,
    )
    return (result, input_grad.astype(jnp.bfloat16))


MESH = pl.DeviceIdType.MESH
SUBLANES = 8
LANES = 128
ROWS = 32
VMEM_LIMIT = 60 * 1024 * 1024


def vmem_specs(count):
    return [pl.BlockSpec(memory_space=pltpu.VMEM)] * count


def square_partners():
    me = lax.axis_index("tp")
    y, x = me // 2, me % 2
    return me, y * 2 + (1 - x), (1 - y) * 2 + x, (1 - y) * 2 + (1 - x)


def announce(axis, partners):
    barrier = pltpu.get_barrier_semaphore()
    for partner in partners:
        pl.semaphore_signal(barrier, inc=1, device_id={axis: partner}, device_id_type=MESH)
    return lambda: pl.semaphore_wait(barrier, len(partners))


def greet(axis, partners):
    announce(axis, partners)()


def project_kernel(tok_ref, w_hbm, out_ref, held, w_buf, w_sem, send_sem, recv_sem):
    rows = tok_ref.shape[0]
    half, part_rows = rows // 2, rows // 4
    width = w_hbm.shape[2]
    tile = w_buf.shape[2]
    per_stream = width // tile
    me, xn, yn, dg = square_partners()
    loads = []
    for part in range(3 * per_stream):
        stream, col = divmod(part, per_stream)
        load = pltpu.make_async_copy(
            w_hbm.at[stream, :, pl.ds(col * tile, tile)], w_buf.at[part], w_sem.at[part]
        )
        load.start()
        loads.append(load)
    greet("tp", (xn, yn))

    def send(index, source, slot, start, partner):
        return pltpu.make_async_remote_copy(
            src_ref=source,
            dst_ref=held.at[slot, pl.ds(start, source.shape[0])],
            send_sem=send_sem.at[index],
            recv_sem=recv_sem.at[index],
            device_id={"tp": partner},
            device_id_type=MESH,
        )

    own_a, own_b = tok_ref.at[pl.ds(0, half)], tok_ref.at[pl.ds(half, half)]
    copies = [
        send(0, own_a, 0, 0, xn),
        send(1, own_b, 1, half, yn),
        send(2, own_b, 0, half, xn),
        send(3, own_a, 1, 0, yn),
        send(4, held.at[0, pl.ds(0, part_rows)], 2, 0, yn),
        send(5, held.at[1, pl.ds(half, part_rows)], 2, part_rows, xn),
        send(6, held.at[0, pl.ds(part_rows, part_rows)], 2, half, yn),
        send(7, held.at[1, pl.ds(half + part_rows, part_rows)], 2, half + part_rows, xn),
    ]
    for index in range(4):
        copies[index].start()

    def multiply(block, owner):
        start = pl.multiple_of(owner * rows, rows)

        @pl.loop(0, 3 * per_stream)
        def _(part):
            out_ref[part, pl.ds(start, rows), :] = jnp.dot(
                block[...], w_buf[part], preferred_element_type=jnp.float32
            ).astype(out_ref.dtype)

    for load in loads:
        load.wait()
    multiply(tok_ref, me)
    copies[0].wait_recv()
    copies[4].start()
    copies[6].start()
    copies[1].wait_recv()
    copies[5].start()
    copies[7].start()
    copies[2].wait_recv()
    multiply(held.at[0], xn)
    copies[3].wait_recv()
    multiply(held.at[1], yn)
    for step in range(2):
        copies[4 + 2 * step].wait_recv()
        copies[5 + 2 * step].wait_recv()
        upper = pl.multiple_of(dg * rows + step * part_rows, part_rows)
        lower = pl.multiple_of(dg * rows + half + step * part_rows, part_rows)
        block = held.at[2, pl.ds(step * half, half)]

        @pl.loop(0, 3 * per_stream)
        def _(part, block=block, upper=upper, lower=lower):
            value = jnp.dot(
                block[...], w_buf[part], preferred_element_type=jnp.float32
            ).astype(out_ref.dtype)
            out_ref[part, pl.ds(upper, part_rows), :] = value[:part_rows]
            out_ref[part, pl.ds(lower, part_rows), :] = value[part_rows:]

    for copy in copies:
        copy.wait_send()


def gather_project(tokens, in_weight):
    rows, depth = tokens.shape
    streams, _, width = in_weight.shape
    tile = min(256, width)
    parts = streams * (width // tile)
    return pl.pallas_call(
        project_kernel,
        out_shape=jax.ShapeDtypeStruct((parts, 4 * rows, tile), jnp.bfloat16),
        in_specs=[pl.BlockSpec(memory_space=pltpu.VMEM), pl.BlockSpec(memory_space=pl.ANY)],
        out_specs=pl.BlockSpec(memory_space=pltpu.VMEM),
        scratch_shapes=[
            pltpu.VMEM((3, rows, depth), jnp.bfloat16),
            pltpu.VMEM((parts, depth, tile), jnp.bfloat16),
            pltpu.SemaphoreType.DMA((parts,)),
            pltpu.SemaphoreType.DMA((8,)),
            pltpu.SemaphoreType.DMA((8,)),
        ],
        compiler_params=pltpu.CompilerParams(
            collective_id=0, has_side_effects=True, vmem_limit_bytes=VMEM_LIMIT
        ),
    )(tokens, in_weight)


def tree_sum(values):
    while len(values) > 1:
        values = [a + b for a, b in zip(values[::2], values[1::2])] + (
            [values[-1]] if len(values) % 2 else []
        )
    return values[0]


def middle_kernel(
    count, st_ref, taps_ref, rate_ref, res_ref, skip_ref, grad_ref, mixed_ref, gs_ref,
    ext, side, prod, cgrad, conv, back, sgrad, halo, pole, carry_f, carry_b,
    mine_f, mine_b, all_f, all_b, inc_f, inc_b,
    send_f, recv_f, send_b, recv_b, send_h, recv_h,
):
    parts, length, tile = st_ref.shape
    width = mixed_ref.shape[1]
    per_stream = width // tile
    modes = rate_ref.shape[0]
    section = length // SUBLANES
    chunks = length // ROWS
    me = lax.axis_index("ctx")
    after, prior = lax.rem(me + 1, count), lax.rem(me + count - 1, count)
    entered = announce("ctx", [lax.rem(me + step, count) for step in range(1, count)])

    def neighbour(index, source, target, partner):
        return pltpu.make_async_remote_copy(
            src_ref=source,
            dst_ref=target,
            send_sem=send_h.at[index],
            recv_sem=recv_h.at[index],
            device_id={"ctx": partner},
            device_id_type=MESH,
        )

    first = neighbour(0, st_ref.at[:, pl.ds(length - 16, 16), :], halo, after)
    pole[...] = jnp.exp(-rate_ref[...])

    @pl.loop(0, chunks)
    def _(step):
        start = pl.multiple_of(step * ROWS, ROWS)
        for part in range(parts):
            ext[pl.ds(start + 8, ROWS), part * tile : (part + 1) * tile] = st_ref[
                part, pl.ds(start, ROWS), :
            ].astype(jnp.float32)

    entered()
    first.start()

    def short_mix(start):
        for col in range(0, width, LANES):
            lanes = slice(col, col + LANES)
            mixed = []
            for s in range(3):
                block = ext[pl.ds(start, ROWS + 8), s * width + col : s * width + col + LANES]
                value = taps_ref[s, 0:1, lanes] * block[8:]
                for j in range(1, 3):
                    value = value + taps_ref[s, j : j + 1, lanes] * block[8 - j : 8 - j + ROWS]
                side[s, pl.ds(start, ROWS), lanes] = value
                mixed.append(value)
            prod[col // LANES, pl.ds(start, ROWS), :] = mixed[1] * mixed[2]
            cgrad[col // LANES, pl.ds(start, ROWS), :] = (
                grad_ref[pl.ds(start, ROWS), lanes].astype(jnp.float32) * mixed[0]
            )

    @pl.loop(1, chunks)
    def _(step):
        short_mix(pl.multiple_of(step * ROWS, ROWS))

    first.wait_recv()
    keep = jnp.where(me > 0, 1.0, 0.0).astype(jnp.float32)
    for part in range(parts):
        ext[0:8, part * tile : (part + 1) * tile] = (
            halo[part].astype(jnp.float32)[8:16] * keep
        )

    short_mix(0)

    tiles = width // LANES
    sub = lax.broadcasted_iota(jnp.int32, (SUBLANES, LANES), 0)

    def wide(ref, lanes):
        return [
            jnp.broadcast_to(ref[n : n + 1, lanes], (SUBLANES, LANES)) for n in range(modes)
        ]

    def end_states(source, carry, mine, reverse):
        @pl.loop(0, tiles)
        def _(t):
            lanes = pl.ds(pl.multiple_of(t * LANES, LANES), LANES)
            p = wide(pole, lanes)

            def body(i, state):
                j = section - 1 - i if reverse else i
                x = source[t, pl.ds(j, SUBLANES, stride=section), :]
                return [a * b + x for a, b in zip(p, state)]

            zero = jnp.zeros((SUBLANES, LANES), jnp.float32)
            ends = lax.fori_loop(0, section, body, [zero] * modes, unroll=4)
            for n in range(modes):
                rate = rate_ref[n : n + 1, lanes]
                total = ends[n] * res_ref[n : n + 1, lanes]
                for k in (1, 2, 4):
                    decay = jnp.exp(rate * (-1.0 * section * k))
                    moved = pltpu.roll(total, SUBLANES - k if reverse else k, 0)
                    inside = sub < SUBLANES - k if reverse else sub >= k
                    total = total + jnp.where(inside, decay * moved, 0.0)
                moved = pltpu.roll(total, SUBLANES - 1 if reverse else 1, 0)
                inside = sub < SUBLANES - 1 if reverse else sub >= 1
                carry[n, :, lanes] = jnp.where(inside, moved, 0.0)
                mine[n : n + 1, lanes] = total[0:1] if reverse else total[SUBLANES - 1 :]

    def local_scan(source, target, carry, reverse):
        @pl.loop(0, tiles)
        def _(t):
            lanes = pl.ds(pl.multiple_of(t * LANES, LANES), LANES)
            p, r = wide(pole, lanes), wide(res_ref, lanes)

            def body(i, state):
                j = section - 1 - i if reverse else i
                x = source[t, pl.ds(j, SUBLANES, stride=section), :]
                state = [a * b + c * x for a, b, c in zip(p, state, r)]
                target[t, pl.ds(j, SUBLANES, stride=section), :] = tree_sum(state)
                return state

            start = [carry[n, :, lanes] for n in range(modes)]
            lax.fori_loop(0, section, body, start, unroll=2)

    def summary(mine, table, send_sem, recv_sem, source, partner):
        return pltpu.make_async_remote_copy(
            src_ref=mine,
            dst_ref=table.at[source],
            send_sem=send_sem.at[partner],
            recv_sem=recv_sem.at[source],
            device_id={"ctx": partner},
            device_id_type=MESH,
        )

    forward = functools.partial(summary, mine_f, all_f, send_f, recv_f)
    backward = functools.partial(summary, mine_b, all_b, send_b, recv_b)

    end_states(prod, carry_f, mine_f, False)
    for other in range(count):

        @pl.when(other > me)
        def _(other=other):
            forward(me, other).start()

    end_states(cgrad, carry_b, mine_b, True)
    for other in range(count):

        @pl.when(other < me)
        def _(other=other):
            backward(me, other).start()

    local_scan(prod, conv, carry_f, False)
    local_scan(cgrad, back, carry_b, True)

    def add_carry(target, incoming, reverse):
        @pl.loop(0, tiles)
        def _(t):
            lanes = pl.ds(pl.multiple_of(t * LANES, LANES), LANES)
            p = wide(pole, lanes)
            steps = (SUBLANES - 1 - sub if reverse else sub).astype(jnp.float32) * (-1.0 * section)
            state = [
                jnp.exp(rate_ref[n : n + 1, lanes] * steps) * incoming[n : n + 1, lanes]
                for n in range(modes)
            ]

            def body(i, state):
                j = section - 1 - i if reverse else i
                state = [a * b for a, b in zip(p, state)]
                place = pl.ds(j, SUBLANES, stride=section)
                target[t, place, :] = target[t, place, :] + tree_sum(state)
                return state

            lax.fori_loop(0, section, body, state, unroll=2)

    inc_f[...] = jnp.zeros_like(inc_f)
    for other in range(count):

        @pl.when(other < me)
        def _(other=other):
            forward(other, me).wait_recv()
            gap = ((other + 1 - me) * length).astype(jnp.float32)
            inc_f[...] += jnp.exp(rate_ref[...] * gap) * all_f[other]

    add_carry(conv, inc_f, False)
    inc_b[...] = jnp.zeros_like(inc_b)
    for other in range(count):

        @pl.when(other > me)
        def _(other=other):
            backward(other, me).wait_recv()
            gap = ((me + 1 - other) * length).astype(jnp.float32)
            inc_b[...] += jnp.exp(rate_ref[...] * gap) * all_b[other]

    add_carry(back, inc_b, True)

    def finish(start):
        for col in range(0, width, LANES):
            lanes = slice(col, col + LANES)
            rows = pl.ds(start, ROWS)
            skip = skip_ref[0:1, lanes]
            filtered = conv[col // LANES, rows, :] + skip * prod[col // LANES, rows, :]
            mixed_ref[rows, lanes] = (side[0, rows, lanes] * filtered).astype(mixed_ref.dtype)
            product = back[col // LANES, rows, :] + skip * cgrad[col // LANES, rows, :]
            upstream = grad_ref[rows, lanes].astype(jnp.float32)
            sgrad[rows, lanes] = upstream * filtered
            sgrad[rows, width + col : width + col + LANES] = product * side[2, rows, lanes]
            sgrad[rows, 2 * width + col : 2 * width + col + LANES] = product * side[1, rows, lanes]

    finish(0)
    last = neighbour(1, sgrad.at[pl.ds(0, 8)], sgrad.at[pl.ds(length, 8)], prior)
    last.start()

    @pl.loop(1, chunks)
    def _(step):
        finish(pl.multiple_of(step * ROWS, ROWS))

    def transpose_taps(start):
        for s in range(3):
            for col in range(0, width, LANES):
                lanes = slice(s * width + col, s * width + col + LANES)
                block = sgrad[pl.ds(start, ROWS + 8), lanes]
                value = taps_ref[s, 0:1, col : col + LANES] * block[:ROWS]
                for j in range(1, 3):
                    value = value + taps_ref[s, j : j + 1, col : col + LANES] * block[j : j + ROWS]
                gs_ref[pl.ds(start, ROWS), lanes] = value.astype(gs_ref.dtype)

    @pl.loop(0, chunks - 1)
    def _(step):
        transpose_taps(pl.multiple_of(step * ROWS, ROWS))

    last.wait_recv()

    @pl.when(me == count - 1)
    def _():
        sgrad[length : length + 8, :] = jnp.zeros((8, 3 * width), jnp.float32)

    transpose_taps(length - ROWS)
    first.wait_send()
    last.wait_send()
    for other in range(count):

        @pl.when(other > me)
        def _(other=other):
            forward(me, other).wait_send()

        @pl.when(other < me)
        def _(other=other):
            backward(me, other).wait_send()


def middle(streams, short_taps, decay_rate, residue, skip_gain, grad_out):
    count = lax.axis_size("ctx")
    parts, length, tile = streams.shape
    modes, width = decay_rate.shape
    f32 = jnp.float32
    table = pltpu.VMEM((modes, width), f32)
    tables = pltpu.VMEM((count, modes, width), f32)
    plane = pltpu.VMEM((width // LANES, length, LANES), f32)
    carry = pltpu.VMEM((modes, SUBLANES, width), f32)
    dma = pltpu.SemaphoreType.DMA
    return pl.pallas_call(
        functools.partial(middle_kernel, count),
        out_shape=(
            jax.ShapeDtypeStruct((length, width), jnp.bfloat16),
            jax.ShapeDtypeStruct((length, 3 * width), jnp.bfloat16),
        ),
        in_specs=vmem_specs(6),
        out_specs=tuple(vmem_specs(2)),
        scratch_shapes=[
            pltpu.VMEM((length + 8, 3 * width), f32),
            pltpu.VMEM((3, length, width), f32),
            plane, plane, plane, plane,
            pltpu.VMEM((length + 8, 3 * width), f32),
            pltpu.VMEM((parts, 16, tile), jnp.bfloat16),
            table, carry, carry, table, table, tables, tables, table, table,
            dma((count,)), dma((count,)), dma((count,)), dma((count,)), dma((2,)), dma((2,)),
        ],
        compiler_params=pltpu.CompilerParams(
            collective_id=1, has_side_effects=True, vmem_limit_bytes=VMEM_LIMIT
        ),
    )(streams, short_taps, decay_rate, residue, skip_gain[None], grad_out)


def scatter_kernel(gs_ref, w_hbm, out_ref, w_buf, out_buf, in_buf, own, w_sem, send_sem, recv_sem):
    rows, depth = out_ref.shape
    pieces, streams, cols, width = w_buf.shape
    half = pieces // 2
    me, xn, yn, dg = square_partners()

    def load(piece):
        return pltpu.make_async_copy(
            w_hbm.at[:, pl.ds(piece * cols, cols), :], w_buf.at[piece], w_sem.at[piece]
        )

    for piece in range(half):
        load(piece).start()
        load(half + piece).start()
    entered = announce("tp", (xn, yn))

    def send(kind, piece, partner):
        return pltpu.make_async_remote_copy(
            src_ref=out_buf.at[kind, piece],
            dst_ref=in_buf.at[kind, piece],
            send_sem=send_sem.at[kind, piece],
            recv_sem=recv_sem.at[kind, piece],
            device_id={"tp": partner},
            device_id_type=MESH,
        )

    def partial(owner, piece):
        block = pl.ds(pl.multiple_of(owner * rows, rows), rows)
        total = None
        for s in range(streams):
            term = lax.dot_general(
                gs_ref[block, s * width : (s + 1) * width],
                w_buf[piece, s],
                (((1,), (1,)), ((), ())),
                preferred_element_type=jnp.float32,
            )
            total = term if total is None else total + term
        return total

    def emit(kind, piece, value, partner):
        out_buf[kind, piece] = value.astype(out_buf.dtype)
        send(kind, piece, partner).start()

    load(0).wait()
    opening = partial(dg, 0)
    entered()
    emit(0, 0, opening, xn)
    load(half).wait()
    emit(0, half, partial(dg, half), yn)

    @pl.loop(1, half)
    def _(k):
        load(k).wait()
        emit(0, k, partial(dg, k), xn)
        load(half + k).wait()
        emit(0, half + k, partial(dg, half + k), yn)

    @pl.loop(0, half)
    def _(k):
        emit(1, k, partial(xn, k), xn)
        emit(2, half + k, partial(yn, half + k), yn)

    @pl.loop(0, half)
    def _(k):
        own_x, own_y = partial(xn, half + k), partial(yn, k)
        send(0, half + k, yn).wait_recv()
        emit(1, half + k, own_x + in_buf[0, half + k].astype(jnp.float32), xn)
        send(0, k, xn).wait_recv()
        emit(2, k, own_y + in_buf[0, k].astype(jnp.float32), yn)

    @pl.loop(0, pieces)
    def _(k):
        own[k] = partial(me, k)

    for k in [k + offset for k in range(half) for offset in (0, half)]:
        send(1, k, xn).wait_recv()
        send(2, k, yn).wait_recv()
        out_ref[:, k * cols : (k + 1) * cols] = (
            own[k] + in_buf[1, k].astype(jnp.float32) + in_buf[2, k].astype(jnp.float32)
        ).astype(out_ref.dtype)
    for k in range(pieces):
        send(0, k, xn if k < half else yn).wait_send()
        send(1, k, xn).wait_send()
        send(2, k, yn).wait_send()


def project_back(grad_streams, in_weight):
    length = grad_streams.shape[0]
    streams, depth, width = in_weight.shape
    rows, pieces = length // 4, 8
    cols = depth // pieces
    travelling = pltpu.VMEM((3, pieces, rows, cols), jnp.bfloat16)
    return pl.pallas_call(
        scatter_kernel,
        out_shape=jax.ShapeDtypeStruct((rows, depth), jnp.bfloat16),
        in_specs=[pl.BlockSpec(memory_space=pltpu.VMEM), pl.BlockSpec(memory_space=pl.ANY)],
        out_specs=pl.BlockSpec(memory_space=pltpu.VMEM),
        scratch_shapes=[
            pltpu.VMEM((pieces, streams, cols, width), jnp.bfloat16),
            travelling,
            travelling,
            pltpu.VMEM((pieces, rows, cols), jnp.float32),
            pltpu.SemaphoreType.DMA((pieces,)),
            pltpu.SemaphoreType.DMA((3, pieces)),
            pltpu.SemaphoreType.DMA((3, pieces)),
        ],
        compiler_params=pltpu.CompilerParams(
            collective_id=2, has_side_effects=True, vmem_limit_bytes=VMEM_LIMIT
        ),
    )(grad_streams, in_weight)


def square_shards(tokens, in_weight, short_taps, decay_rate, residue, skip_gain, grad_out):
    streams = gather_project(tokens, in_weight)
    mixed_out, grad_streams = middle(
        streams, short_taps, decay_rate, residue, skip_gain, grad_out
    )
    return mixed_out, project_back(grad_streams, in_weight)


def solution(mesh):
    in_specs = (
        P(("ctx", "tp"), None),
        P(None, None, "tp"),
        P(None, None, "tp"),
        P(None, "tp"),
        P(None, "tp"),
        P("tp"),
        P("ctx", "tp"),
    )
    out_specs = (P("ctx", "tp"), P(("ctx", "tp"), None))
    body = square_shards if mesh.shape["tp"] == 4 else shards
    return jax.shard_map(body, mesh=mesh, in_specs=in_specs, out_specs=out_specs, check_vma=False)
```

```python
import functools

import jax
import jax.numpy as jnp
from jax import lax
from jax.experimental import pallas as pl
from jax.experimental.pallas import tpu as pltpu
from jax.sharding import PartitionSpec as P

exact_mode = lax.Precision.HIGHEST


def from_behind(value, axis, steps):
    count = lax.axis_size(axis)
    leading, last = (max(0, -steps), min(count, count - steps))
    return lax.ppermute(value, axis, [(source, source + steps) for source in range(leading, last)])


def modal_block(signal, log_pole, residue):
    length, channels = signal.shape
    sub_len = min(64, length)
    sub_count = length // sub_len
    offsets = jnp.arange(sub_len, dtype=jnp.float32)
    sections = signal.reshape(sub_count, sub_len, channels)
    powers = jnp.exp(log_pole[:, None, :] * offsets[None, :, None])
    filter_taps = jnp.sum(residue[:, None, :] * powers, axis=0)
    lag_index = jnp.arange(sub_len)[:, None] - jnp.arange(sub_len)[None, :]
    toeplitz = jnp.where((lag_index >= 0)[:, :, None], filter_taps[jnp.maximum(lag_index, 0)], 0.0)
    within = jnp.einsum("abc,kbc->kac", toeplitz, sections, precision=exact_mode)
    to_end = jnp.exp(log_pole[:, None, :] * (sub_len - 1.0 - offsets)[None, :, None])
    end_states = jnp.einsum("nbc,kbc->nkc", to_end, sections, precision=exact_mode)
    lag_blocks = jnp.arange(sub_count + 1)[:, None] - 1 - jnp.arange(sub_count)[None, :]
    valid_lag = lag_blocks >= 0
    lag_float = (jnp.maximum(lag_blocks, 0) * sub_len).astype(jnp.float32)
    decay_table = jnp.exp(log_pole[None, None] * lag_float[:, :, None, None])
    decay_table = jnp.where(valid_lag[:, :, None, None], decay_table, 0.0)
    carried = jnp.einsum("kmnc,nmc->nkc", decay_table, end_states, precision=exact_mode)
    stepped = residue[:, None, :] * jnp.exp(log_pole[:, None, :] * (offsets[None, :, None] + 1.0))
    output = within + jnp.einsum(
        "nac,nkc->kac", stepped, carried[:, :sub_count], precision=exact_mode
    )
    return (output.reshape(length, channels), carried[:, sub_count])


def carry_term(incoming, log_pole, residue, length):
    channels = incoming.shape[1]
    sub_len = min(64, length)
    sub_count = length // sub_len
    offsets = jnp.arange(sub_len, dtype=jnp.float32)
    stepped = residue[:, None, :] * jnp.exp(log_pole[:, None, :] * (offsets[None, :, None] + 1.0))
    block_starts = (jnp.arange(sub_count) * sub_len).astype(jnp.float32)
    start_states = incoming[:, None, :] * jnp.exp(
        log_pole[:, None, :] * block_starts[None, :, None]
    )
    output = jnp.einsum("nac,nkc->kac", stepped, start_states, precision=exact_mode)
    return output.reshape(length, channels)


def shards(tokens, in_weight, short_taps, decay_rate, residue, skip_gain, grad_out):
    width = in_weight.shape[2]
    weight_cat = jnp.concatenate([in_weight[0], in_weight[1], in_weight[2]], axis=1)
    streams = jnp.dot(
        lax.all_gather(tokens, "tp", axis=0, tiled=True),
        weight_cat,
        preferred_element_type=jnp.float32,
    ).astype(jnp.bfloat16)
    length = streams.shape[0]
    tap_reach = short_taps.shape[1] - 1
    taps_cat = jnp.concatenate([short_taps[0], short_taps[1], short_taps[2]], axis=1)
    before = from_behind(streams[length - tap_reach :], "ctx", 1)
    extended = jnp.concatenate([before, streams], axis=0).astype(jnp.float32)
    short_mixed = taps_cat[0][None] * extended[tap_reach:]
    for offset in range(1, tap_reach + 1):
        short_mixed = (
            short_mixed
            + taps_cat[offset][None] * extended[tap_reach - offset : tap_reach - offset + length]
        )
    query_side = short_mixed[:, :width]
    key_side = short_mixed[:, width : 2 * width]
    value_side = short_mixed[:, 2 * width :]
    product_in = key_side * value_side
    log_pole = -decay_rate
    forward_local, forward_sum = modal_block(product_in, log_pole, residue)
    upstream = grad_out.astype(jnp.float32)
    conv_grad = upstream * query_side
    backward_local, backward_sum = modal_block(conv_grad[::-1], log_pole, residue)
    position = lax.axis_index("ctx")
    summaries = (
        lax.all_gather(forward_sum[None], "ctx", axis=0, tiled=True),
        lax.all_gather(backward_sum[None], "ctx", axis=0, tiled=True),
    )
    block_index = jnp.arange(summaries[0].shape[0])
    earlier_gap = position - 1 - block_index
    later_gap = block_index - position - 1
    scale_fwd = (jnp.maximum(earlier_gap, 0) * length).astype(jnp.float32)
    scale_bwd = (jnp.maximum(later_gap, 0) * length).astype(jnp.float32)
    weight_fwd = jnp.where(
        (earlier_gap >= 0)[:, None, None], jnp.exp(log_pole[None] * scale_fwd[:, None, None]), 0.0
    )
    weight_bwd = jnp.where(
        (later_gap >= 0)[:, None, None], jnp.exp(log_pole[None] * scale_bwd[:, None, None]), 0.0
    )
    incoming_fwd = jnp.sum(weight_fwd * summaries[0], axis=0)
    incoming_bwd = jnp.sum(weight_bwd * summaries[1], axis=0)
    conv_out = forward_local + carry_term(incoming_fwd, log_pole, residue, length)
    back_conv = (backward_local + carry_term(incoming_bwd, log_pole, residue, length))[::-1]
    filtered = conv_out + skip_gain[None] * product_in
    result = (query_side * filtered).astype(jnp.bfloat16)
    grad_query = upstream * filtered
    grad_product = back_conv + skip_gain[None] * conv_grad
    stream_grads = jnp.concatenate(
        [grad_query, grad_product * value_side, grad_product * key_side], axis=1
    )
    after_rows = from_behind(stream_grads[:tap_reach], "ctx", -1)
    padded = jnp.concatenate([stream_grads, after_rows], axis=0)
    grad_streams = taps_cat[0][None] * padded[:length]
    for offset in range(1, tap_reach + 1):
        grad_streams = grad_streams + taps_cat[offset][None] * padded[offset : offset + length]
    grad_streams = grad_streams.astype(jnp.bfloat16)
    input_grad = lax.psum_scatter(
        jnp.einsum("rk,dk->rd", grad_streams, weight_cat, preferred_element_type=jnp.float32),
        "tp",
        scatter_dimension=0,
        tiled=True,
    )
    return (result, input_grad.astype(jnp.bfloat16))


MESH = pl.DeviceIdType.MESH
SUBLANES = 8
LANES = 128
ROWS = 32
VMEM_LIMIT = 60 * 1024 * 1024


def vmem_specs(count):
    return [pl.BlockSpec(memory_space=pltpu.VMEM)] * count


def square_partners():
    me = lax.axis_index("tp")
    y, x = me // 2, me % 2
    return me, y * 2 + (1 - x), (1 - y) * 2 + x, (1 - y) * 2 + (1 - x)


def announce(axis, partners):
    barrier = pltpu.get_barrier_semaphore()
    for partner in partners:
        pl.semaphore_signal(barrier, inc=1, device_id={axis: partner}, device_id_type=MESH)
    return lambda: pl.semaphore_wait(barrier, len(partners))


def greet(axis, partners):
    announce(axis, partners)()


def project_kernel(tok_ref, w_hbm, out_ref, held, w_buf, w_sem, send_sem, recv_sem):
    rows = tok_ref.shape[0]
    half, part_rows = rows // 2, rows // 4
    width = w_hbm.shape[2]
    tile = w_buf.shape[2]
    per_stream = width // tile
    me, xn, yn, dg = square_partners()
    loads = []
    for part in range(3 * per_stream):
        stream, col = divmod(part, per_stream)
        load = pltpu.make_async_copy(
            w_hbm.at[stream, :, pl.ds(col * tile, tile)], w_buf.at[part], w_sem.at[part]
        )
        load.start()
        loads.append(load)
    greet("tp", (xn, yn))

    def send(index, source, slot, start, partner):
        return pltpu.make_async_remote_copy(
            src_ref=source,
            dst_ref=held.at[slot, pl.ds(start, source.shape[0])],
            send_sem=send_sem.at[index],
            recv_sem=recv_sem.at[index],
            device_id={"tp": partner},
            device_id_type=MESH,
        )

    own_a, own_b = tok_ref.at[pl.ds(0, half)], tok_ref.at[pl.ds(half, half)]
    copies = [
        send(0, own_a, 0, 0, xn),
        send(1, own_b, 1, half, yn),
        send(2, own_b, 0, half, xn),
        send(3, own_a, 1, 0, yn),
        send(4, held.at[0, pl.ds(0, part_rows)], 2, 0, yn),
        send(5, held.at[1, pl.ds(half, part_rows)], 2, part_rows, xn),
        send(6, held.at[0, pl.ds(part_rows, part_rows)], 2, half, yn),
        send(7, held.at[1, pl.ds(half + part_rows, part_rows)], 2, half + part_rows, xn),
    ]
    for index in range(4):
        copies[index].start()

    def multiply(block, owner):
        start = pl.multiple_of(owner * rows, rows)

        @pl.loop(0, 3 * per_stream)
        def _(part):
            out_ref[part, pl.ds(start, rows), :] = jnp.dot(
                block[...], w_buf[part], preferred_element_type=jnp.float32
            ).astype(out_ref.dtype)

    for load in loads:
        load.wait()
    multiply(tok_ref, me)
    copies[0].wait_recv()
    copies[4].start()
    copies[6].start()
    copies[1].wait_recv()
    copies[5].start()
    copies[7].start()
    copies[2].wait_recv()
    multiply(held.at[0], xn)
    copies[3].wait_recv()
    multiply(held.at[1], yn)
    for step in range(2):
        copies[4 + 2 * step].wait_recv()
        copies[5 + 2 * step].wait_recv()
        upper = pl.multiple_of(dg * rows + step * part_rows, part_rows)
        lower = pl.multiple_of(dg * rows + half + step * part_rows, part_rows)
        block = held.at[2, pl.ds(step * half, half)]

        @pl.loop(0, 3 * per_stream)
        def _(part, block=block, upper=upper, lower=lower):
            value = jnp.dot(
                block[...], w_buf[part], preferred_element_type=jnp.float32
            ).astype(out_ref.dtype)
            out_ref[part, pl.ds(upper, part_rows), :] = value[:part_rows]
            out_ref[part, pl.ds(lower, part_rows), :] = value[part_rows:]

    for copy in copies:
        copy.wait_send()


def gather_project(tokens, in_weight):
    rows, depth = tokens.shape
    streams, _, width = in_weight.shape
    tile = min(256, width)
    parts = streams * (width // tile)
    return pl.pallas_call(
        project_kernel,
        out_shape=jax.ShapeDtypeStruct((parts, 4 * rows, tile), jnp.bfloat16),
        in_specs=[pl.BlockSpec(memory_space=pltpu.VMEM), pl.BlockSpec(memory_space=pl.ANY)],
        out_specs=pl.BlockSpec(memory_space=pltpu.VMEM),
        scratch_shapes=[
            pltpu.VMEM((3, rows, depth), jnp.bfloat16),
            pltpu.VMEM((parts, depth, tile), jnp.bfloat16),
            pltpu.SemaphoreType.DMA((parts,)),
            pltpu.SemaphoreType.DMA((8,)),
            pltpu.SemaphoreType.DMA((8,)),
        ],
        compiler_params=pltpu.CompilerParams(
            collective_id=0, has_side_effects=True, vmem_limit_bytes=VMEM_LIMIT
        ),
    )(tokens, in_weight)


def tree_sum(values):
    while len(values) > 1:
        values = [a + b for a, b in zip(values[::2], values[1::2])] + (
            [values[-1]] if len(values) % 2 else []
        )
    return values[0]


def middle_kernel(
    count, st_ref, taps_ref, rate_ref, res_ref, skip_ref, grad_ref, mixed_ref, gs_ref,
    ext, side, prod, cgrad, conv, back, sgrad, halo, pole, carry_f, carry_b,
    mine_f, mine_b, all_f, all_b, inc_f, inc_b,
    send_f, recv_f, send_b, recv_b, send_h, recv_h,
):
    parts, length, tile = st_ref.shape
    width = mixed_ref.shape[1]
    per_stream = width // tile
    modes = rate_ref.shape[0]
    section = length // SUBLANES
    chunks = length // ROWS
    me = lax.axis_index("ctx")
    after, prior = lax.rem(me + 1, count), lax.rem(me + count - 1, count)
    entered = announce("ctx", [lax.rem(me + step, count) for step in range(1, count)])

    def neighbour(index, source, target, partner):
        return pltpu.make_async_remote_copy(
            src_ref=source,
            dst_ref=target,
            send_sem=send_h.at[index],
            recv_sem=recv_h.at[index],
            device_id={"ctx": partner},
            device_id_type=MESH,
        )

    first = neighbour(0, st_ref.at[:, pl.ds(length - 16, 16), :], halo, after)
    pole[...] = jnp.exp(-rate_ref[...])

    @pl.loop(0, chunks)
    def _(step):
        start = pl.multiple_of(step * ROWS, ROWS)
        for part in range(parts):
            ext[pl.ds(start + 8, ROWS), part * tile : (part + 1) * tile] = st_ref[
                part, pl.ds(start, ROWS), :
            ].astype(jnp.float32)

    entered()
    first.start()

    def short_mix(start):
        for col in range(0, width, LANES):
            lanes = slice(col, col + LANES)
            mixed = []
            for s in range(3):
                block = ext[pl.ds(start, ROWS + 8), s * width + col : s * width + col + LANES]
                value = taps_ref[s, 0:1, lanes] * block[8:]
                for j in range(1, 3):
                    value = value + taps_ref[s, j : j + 1, lanes] * block[8 - j : 8 - j + ROWS]
                side[s, pl.ds(start, ROWS), lanes] = value
                mixed.append(value)
            prod[col // LANES, pl.ds(start, ROWS), :] = mixed[1] * mixed[2]
            cgrad[col // LANES, pl.ds(start, ROWS), :] = (
                grad_ref[pl.ds(start, ROWS), lanes].astype(jnp.float32) * mixed[0]
            )

    @pl.loop(1, chunks)
    def _(step):
        short_mix(pl.multiple_of(step * ROWS, ROWS))

    first.wait_recv()
    keep = jnp.where(me > 0, 1.0, 0.0).astype(jnp.float32)
    for part in range(parts):
        ext[0:8, part * tile : (part + 1) * tile] = (
            halo[part].astype(jnp.float32)[8:16] * keep
        )

    short_mix(0)

    tiles = width // LANES
    sub = lax.broadcasted_iota(jnp.int32, (SUBLANES, LANES), 0)

    def wide(ref, lanes):
        return [
            jnp.broadcast_to(ref[n : n + 1, lanes], (SUBLANES, LANES)) for n in range(modes)
        ]

    def end_states(source, carry, mine, reverse):
        @pl.loop(0, tiles)
        def _(t):
            lanes = pl.ds(pl.multiple_of(t * LANES, LANES), LANES)
            p = wide(pole, lanes)

            def body(i, state):
                j = section - 1 - i if reverse else i
                x = source[t, pl.ds(j, SUBLANES, stride=section), :]
                return [a * b + x for a, b in zip(p, state)]

            zero = jnp.zeros((SUBLANES, LANES), jnp.float32)
            ends = lax.fori_loop(0, section, body, [zero] * modes, unroll=4)
            for n in range(modes):
                rate = rate_ref[n : n + 1, lanes]
                total = ends[n] * res_ref[n : n + 1, lanes]
                for k in (1, 2, 4):
                    decay = jnp.exp(rate * (-1.0 * section * k))
                    moved = pltpu.roll(total, SUBLANES - k if reverse else k, 0)
                    inside = sub < SUBLANES - k if reverse else sub >= k
                    total = total + jnp.where(inside, decay * moved, 0.0)
                moved = pltpu.roll(total, SUBLANES - 1 if reverse else 1, 0)
                inside = sub < SUBLANES - 1 if reverse else sub >= 1
                carry[n, :, lanes] = jnp.where(inside, moved, 0.0)
                mine[n : n + 1, lanes] = total[0:1] if reverse else total[SUBLANES - 1 :]

    def incoming_at(incoming, lanes, reverse):
        steps = (SUBLANES - 1 - sub if reverse else sub).astype(jnp.float32) * (-1.0 * section)
        return [
            jnp.exp(rate_ref[n : n + 1, lanes] * steps) * incoming[n : n + 1, lanes]
            for n in range(modes)
        ]

    def local_scan(source, target, carry, incoming, reverse):
        @pl.loop(0, tiles)
        def _(t):
            lanes = pl.ds(pl.multiple_of(t * LANES, LANES), LANES)
            p, r = wide(pole, lanes), wide(res_ref, lanes)

            def body(i, state):
                j = section - 1 - i if reverse else i
                x = source[t, pl.ds(j, SUBLANES, stride=section), :]
                state = [a * b + c * x for a, b, c in zip(p, state, r)]
                target[t, pl.ds(j, SUBLANES, stride=section), :] = tree_sum(state)
                return state

            start = [carry[n, :, lanes] for n in range(modes)]
            if incoming is not None:
                arrived = incoming_at(incoming, lanes, reverse)
                start = [a + b for a, b in zip(start, arrived)]
            lax.fori_loop(0, section, body, start, unroll=2)

    def summary(mine, table, send_sem, recv_sem, source, partner):
        return pltpu.make_async_remote_copy(
            src_ref=mine,
            dst_ref=table.at[source],
            send_sem=send_sem.at[partner],
            recv_sem=recv_sem.at[source],
            device_id={"ctx": partner},
            device_id_type=MESH,
        )

    forward = functools.partial(summary, mine_f, all_f, send_f, recv_f)
    backward = functools.partial(summary, mine_b, all_b, send_b, recv_b)

    end_states(cgrad, carry_b, mine_b, True)
    for other in range(count):

        @pl.when(other < me)
        def _(other=other):
            backward(me, other).start()

    end_states(prod, carry_f, mine_f, False)
    for other in range(count):

        @pl.when(other > me)
        def _(other=other):
            forward(me, other).start()

    local_scan(prod, conv, carry_f, None, False)

    def add_carry(target, incoming, reverse):
        @pl.loop(0, tiles)
        def _(t):
            lanes = pl.ds(pl.multiple_of(t * LANES, LANES), LANES)
            p = wide(pole, lanes)
            state = incoming_at(incoming, lanes, reverse)

            def body(i, state):
                j = section - 1 - i if reverse else i
                state = [a * b for a, b in zip(p, state)]
                place = pl.ds(j, SUBLANES, stride=section)
                target[t, place, :] = target[t, place, :] + tree_sum(state)
                return state

            lax.fori_loop(0, section, body, state, unroll=2)

    inc_b[...] = jnp.zeros_like(inc_b)
    for other in range(count):

        @pl.when(other > me)
        def _(other=other):
            backward(other, me).wait_recv()
            gap = ((me + 1 - other) * length).astype(jnp.float32)
            inc_b[...] += jnp.exp(rate_ref[...] * gap) * all_b[other]

    local_scan(cgrad, back, carry_b, inc_b, True)
    inc_f[...] = jnp.zeros_like(inc_f)
    for other in range(count):

        @pl.when(other < me)
        def _(other=other):
            forward(other, me).wait_recv()
            gap = ((other + 1 - me) * length).astype(jnp.float32)
            inc_f[...] += jnp.exp(rate_ref[...] * gap) * all_f[other]

    add_carry(conv, inc_f, False)


    def finish(start):
        for col in range(0, width, LANES):
            lanes = slice(col, col + LANES)
            rows = pl.ds(start, ROWS)
            skip = skip_ref[0:1, lanes]
            filtered = conv[col // LANES, rows, :] + skip * prod[col // LANES, rows, :]
            mixed_ref[rows, lanes] = (side[0, rows, lanes] * filtered).astype(mixed_ref.dtype)
            product = back[col // LANES, rows, :] + skip * cgrad[col // LANES, rows, :]
            upstream = grad_ref[rows, lanes].astype(jnp.float32)
            sgrad[rows, lanes] = upstream * filtered
            sgrad[rows, width + col : width + col + LANES] = product * side[2, rows, lanes]
            sgrad[rows, 2 * width + col : 2 * width + col + LANES] = product * side[1, rows, lanes]

    finish(0)
    last = neighbour(1, sgrad.at[pl.ds(0, 8)], sgrad.at[pl.ds(length, 8)], prior)
    last.start()

    @pl.loop(1, chunks)
    def _(step):
        finish(pl.multiple_of(step * ROWS, ROWS))

    def transpose_taps(start):
        for s in range(3):
            for col in range(0, width, LANES):
                lanes = slice(s * width + col, s * width + col + LANES)
                block = sgrad[pl.ds(start, ROWS + 8), lanes]
                value = taps_ref[s, 0:1, col : col + LANES] * block[:ROWS]
                for j in range(1, 3):
                    value = value + taps_ref[s, j : j + 1, col : col + LANES] * block[j : j + ROWS]
                gs_ref[pl.ds(start, ROWS), lanes] = value.astype(gs_ref.dtype)

    @pl.loop(0, chunks - 1)
    def _(step):
        transpose_taps(pl.multiple_of(step * ROWS, ROWS))

    last.wait_recv()

    @pl.when(me == count - 1)
    def _():
        sgrad[length : length + 8, :] = jnp.zeros((8, 3 * width), jnp.float32)

    transpose_taps(length - ROWS)
    first.wait_send()
    last.wait_send()
    for other in range(count):

        @pl.when(other > me)
        def _(other=other):
            forward(me, other).wait_send()

        @pl.when(other < me)
        def _(other=other):
            backward(me, other).wait_send()


def middle(streams, short_taps, decay_rate, residue, skip_gain, grad_out):
    count = lax.axis_size("ctx")
    parts, length, tile = streams.shape
    modes, width = decay_rate.shape
    f32 = jnp.float32
    table = pltpu.VMEM((modes, width), f32)
    tables = pltpu.VMEM((count, modes, width), f32)
    plane = pltpu.VMEM((width // LANES, length, LANES), f32)
    carry = pltpu.VMEM((modes, SUBLANES, width), f32)
    dma = pltpu.SemaphoreType.DMA
    return pl.pallas_call(
        functools.partial(middle_kernel, count),
        out_shape=(
            jax.ShapeDtypeStruct((length, width), jnp.bfloat16),
            jax.ShapeDtypeStruct((length, 3 * width), jnp.bfloat16),
        ),
        in_specs=vmem_specs(6),
        out_specs=tuple(vmem_specs(2)),
        scratch_shapes=[
            pltpu.VMEM((length + 8, 3 * width), f32),
            pltpu.VMEM((3, length, width), f32),
            plane, plane, plane, plane,
            pltpu.VMEM((length + 8, 3 * width), f32),
            pltpu.VMEM((parts, 16, tile), jnp.bfloat16),
            table, carry, carry, table, table, tables, tables, table, table,
            dma((count,)), dma((count,)), dma((count,)), dma((count,)), dma((2,)), dma((2,)),
        ],
        compiler_params=pltpu.CompilerParams(
            collective_id=1, has_side_effects=True, vmem_limit_bytes=VMEM_LIMIT
        ),
    )(streams, short_taps, decay_rate, residue, skip_gain[None], grad_out)


def scatter_kernel(gs_ref, w_hbm, out_ref, w_buf, out_buf, in_buf, own, w_sem, send_sem, recv_sem):
    rows, depth = out_ref.shape
    pieces, streams, cols, width = w_buf.shape
    half = pieces // 2
    me, xn, yn, dg = square_partners()

    def load(piece):
        return pltpu.make_async_copy(
            w_hbm.at[:, pl.ds(piece * cols, cols), :], w_buf.at[piece], w_sem.at[piece]
        )

    for piece in range(half):
        load(piece).start()
        load(half + piece).start()
    entered = announce("tp", (xn, yn))

    def send(kind, piece, partner):
        return pltpu.make_async_remote_copy(
            src_ref=out_buf.at[kind, piece],
            dst_ref=in_buf.at[kind, piece],
            send_sem=send_sem.at[kind, piece],
            recv_sem=recv_sem.at[kind, piece],
            device_id={"tp": partner},
            device_id_type=MESH,
        )

    def partial(owner, piece):
        block = pl.ds(pl.multiple_of(owner * rows, rows), rows)
        total = None
        for s in range(streams):
            term = lax.dot_general(
                gs_ref[block, s * width : (s + 1) * width],
                w_buf[piece, s],
                (((1,), (1,)), ((), ())),
                preferred_element_type=jnp.float32,
            )
            total = term if total is None else total + term
        return total

    def emit(kind, piece, value, partner):
        out_buf[kind, piece] = value.astype(out_buf.dtype)
        send(kind, piece, partner).start()

    load(0).wait()
    opening = partial(dg, 0)
    entered()
    emit(0, 0, opening, xn)
    load(half).wait()
    emit(0, half, partial(dg, half), yn)

    @pl.loop(1, half)
    def _(k):
        load(k).wait()
        emit(0, k, partial(dg, k), xn)
        load(half + k).wait()
        emit(0, half + k, partial(dg, half + k), yn)

    @pl.loop(0, half)
    def _(k):
        emit(1, k, partial(xn, k), xn)
        emit(2, half + k, partial(yn, half + k), yn)

    @pl.loop(0, half)
    def _(k):
        own_x, own_y = partial(xn, half + k), partial(yn, k)
        send(0, half + k, yn).wait_recv()
        emit(1, half + k, own_x + in_buf[0, half + k].astype(jnp.float32), xn)
        send(0, k, xn).wait_recv()
        emit(2, k, own_y + in_buf[0, k].astype(jnp.float32), yn)

    @pl.loop(0, pieces)
    def _(k):
        own[k] = partial(me, k)

    for k in [k + offset for k in range(half) for offset in (0, half)]:
        send(1, k, xn).wait_recv()
        send(2, k, yn).wait_recv()
        out_ref[:, k * cols : (k + 1) * cols] = (
            own[k] + in_buf[1, k].astype(jnp.float32) + in_buf[2, k].astype(jnp.float32)
        ).astype(out_ref.dtype)
    for k in range(pieces):
        send(0, k, xn if k < half else yn).wait_send()
        send(1, k, xn).wait_send()
        send(2, k, yn).wait_send()


def project_back(grad_streams, in_weight):
    length = grad_streams.shape[0]
    streams, depth, width = in_weight.shape
    rows, pieces = length // 4, 8
    cols = depth // pieces
    travelling = pltpu.VMEM((3, pieces, rows, cols), jnp.bfloat16)
    return pl.pallas_call(
        scatter_kernel,
        out_shape=jax.ShapeDtypeStruct((rows, depth), jnp.bfloat16),
        in_specs=[pl.BlockSpec(memory_space=pltpu.VMEM), pl.BlockSpec(memory_space=pl.ANY)],
        out_specs=pl.BlockSpec(memory_space=pltpu.VMEM),
        scratch_shapes=[
            pltpu.VMEM((pieces, streams, cols, width), jnp.bfloat16),
            travelling,
            travelling,
            pltpu.VMEM((pieces, rows, cols), jnp.float32),
            pltpu.SemaphoreType.DMA((pieces,)),
            pltpu.SemaphoreType.DMA((3, pieces)),
            pltpu.SemaphoreType.DMA((3, pieces)),
        ],
        compiler_params=pltpu.CompilerParams(
            collective_id=2, has_side_effects=True, vmem_limit_bytes=VMEM_LIMIT
        ),
    )(grad_streams, in_weight)


def square_shards(tokens, in_weight, short_taps, decay_rate, residue, skip_gain, grad_out):
    streams = gather_project(tokens, in_weight)
    mixed_out, grad_streams = middle(
        streams, short_taps, decay_rate, residue, skip_gain, grad_out
    )
    return mixed_out, project_back(grad_streams, in_weight)


def solution(mesh):
    in_specs = (
        P(("ctx", "tp"), None),
        P(None, None, "tp"),
        P(None, None, "tp"),
        P(None, "tp"),
        P(None, "tp"),
        P("tp"),
        P("ctx", "tp"),
    )
    out_specs = (P("ctx", "tp"), P(("ctx", "tp"), None))
    body = square_shards if mesh.shape["tp"] == 4 else shards
    return jax.shard_map(body, mesh=mesh, in_specs=in_specs, out_specs=out_specs, check_vma=False)
```
